32 devices in a mesh: groups: 2 (over x), pop: 8 (over z, y), tensor: 2 (over core).
Axes of the slice: x: 2, y: 2, z: 4, core: 2. Of those that a mesh axis runs over, the one named last changes fastest.
Arguments:
- prompts: bfloat16 [48, 8192], P('groups'), parts along dimension 0, may hold values from -6 to 6
- gate_weight: bfloat16 [8192, 14848], P('pop', 'tensor'), may hold values from -0.0625 to 0.0625
- up_weight: bfloat16 [8192, 14848], P('pop', 'tensor'), may hold values from -0.0625 to 0.0625
- down_weight_matrix: bfloat16 [14848, 8192], P('tensor', 'pop'), may hold values from -0.046875 to 0.046875
- gate_in: bfloat16 [16, 8192, 4], P(('groups', 'pop')), parts along dimension 0, may hold values from -6 to 6
- gate_output_factors: bfloat16 [16, 14848, 4], P(('groups', 'pop'), 'tensor'), parts along dimension 0, may hold values from -6 to 6
- up_in: bfloat16 [16, 8192, 4], P(('groups', 'pop')), parts along dimension 0, may hold values from -6 to 6
- up_output_factors: bfloat16 [16, 14848, 4], P(('groups', 'pop'), 'tensor'), parts along dimension 0, may hold values from -6 to 6
- down_input_factors: bfloat16 [16, 14848, 4], P('groups', 'tensor'), parts along dimension 0, may hold values from -6 to 6
- down_out: bfloat16 [16, 8192, 4], P('groups', 'pop'), parts along dimension 0, may hold values from -6 to 6
- label_head: bfloat16 [8192, 128], P('tensor'), may hold values from -0.1875 to 0.1875
- targets: int32 [48], P('groups'), parts along dimension 0, may hold values from 0 to 127
Outputs:
- update: bfloat16 [29696, 8192], P(('groups', 'tensor'), 'pop'), parts along dimension 0
- scores: float32 [16], P(('groups', 'pop')), parts along dimension 0
The draws below stay inside these ranges and needn't reach their ends.
There are 2 independent parts, one for each index of `groups`. The reference program is written for one: setup_inputs(seed, part) draws one part's arguments, and reference() takes and returns one part's arrays. A program takes and returns all parts, laid end to end along the dimension named above; an argument that names none is the same for every part. Nothing has to cross between parts.
All inputs are finite; a program needn't handle non-finite values.
Results may differ from the reference program's by a relative error of at most 0.023.
Values may be sent and summed in bfloat16 or wider, within the bound.
A program may use at most 256 MiB of HBM per device.

```python
import math
import jax
import jax.numpy as jnp
from jax import lax

D = 8192
HIDDEN_UNITS_PART = 14848
RANK = 4
LABELS = 128
ROWS = 24
MEMBERS = 8


def with_ends(drawn, key, smallest, largest):
    place = [jax.random.randint(jax.random.fold_in(key, axis), (), 0, length) for axis, length in enumerate(drawn.shape)]
    widest = drawn.shape.index(max(drawn.shape))
    beside = place[:widest] + [(place[widest] + 1) % drawn.shape[widest]] + place[widest + 1:]
    return drawn.at[tuple(place)].set(smallest).at[tuple(beside)].set(largest)


def shard_levels(rng, dims, split, least, top_value):
    loudness, own = 1.0, jax.random.fold_in(rng, 6)
    for axis_at, parts in split:
        heights = jnp.exp(jax.random.uniform(jax.random.fold_in(own, axis_at), (parts,), jnp.float32, least / len(split), top_value / len(split)))
        loudness = loudness * jnp.repeat(heights, dims[axis_at] // parts).reshape([-1 if axis == axis_at else 1 for axis in range(len(dims))])
    return loudness


def bell_draw(stream_key, dims, scale, bound, pieces=(), held_as=jnp.bfloat16):
    entries = jax.random.normal(stream_key, dims, jnp.float32) * scale
    if len(pieces) > 0:
        entries = shard_levels(stream_key, dims, pieces, -0.22, 0.18) * entries
    return jnp.clip(entries, min=-bound, max=bound).astype(held_as)


def setup_inputs(seed: int = 0, part: int = 0) -> dict:
    keys = jax.random.split(jax.random.key(seed), 13)
    own_keys = jax.random.split(jax.random.fold_in(keys[12], part), 13)
    prompts = bell_draw(own_keys[0], (ROWS, D), 1.0, 6.0)
    gate_weight = bell_draw(keys[1], (D, HIDDEN_UNITS_PART), D ** -0.5, 0.0625, ((0, 8), (1, 2)))
    up_weight = bell_draw(keys[2], (D, HIDDEN_UNITS_PART), D ** -0.5, 0.0625, ((0, 8), (1, 2)))
    down_weight_matrix = bell_draw(keys[3], (HIDDEN_UNITS_PART, D), HIDDEN_UNITS_PART ** -0.5, 0.046875, ((0, 2), (1, 8)))
    gate_in = bell_draw(own_keys[4], (MEMBERS, D, RANK), 1.0, 6.0, ((0, 8),))
    gate_output_factors = bell_draw(own_keys[5], (MEMBERS, HIDDEN_UNITS_PART, RANK), 1.0, 6.0, ((0, 8), (1, 2)))
    up_in = bell_draw(own_keys[6], (MEMBERS, D, RANK), 1.0, 6.0, ((0, 8),))
    up_output_factors = bell_draw(own_keys[7], (MEMBERS, HIDDEN_UNITS_PART, RANK), 1.0, 6.0, ((0, 8), (1, 2)))
    down_input_factors = bell_draw(own_keys[8], (MEMBERS, HIDDEN_UNITS_PART, RANK), 1.0, 6.0, ((1, 2),))
    down_out = bell_draw(own_keys[9], (MEMBERS, D, RANK), 1.0, 6.0, ((1, 8),))
    label_head = bell_draw(keys[10], (D, LABELS), (D // 9) ** -0.5, 0.1875, ((0, 2),))
    targets = with_ends(jax.random.randint(own_keys[11], (ROWS,), 0, LABELS), jax.random.fold_in(own_keys[11], 1), 0, LABELS - 1).astype(jnp.int32)
    return dict(prompts=prompts, gate_weight=gate_weight, up_weight=up_weight, down_weight_matrix=down_weight_matrix, gate_in=gate_in, gate_output_factors=gate_output_factors, up_in=up_in, up_output_factors=up_output_factors, down_input_factors=down_input_factors, down_out=down_out, label_head=label_head, targets=targets)


def scaled_rows(values):
    return values * lax.rsqrt(lax.optimization_barrier(jnp.mean(values * values, axis=-1, keepdims=True)) + 1e-06)

def reference(prompts, gate_weight, up_weight, down_weight_matrix, gate_in, gate_output_factors, up_in, up_output_factors, down_input_factors, down_out, label_head, targets):
    highest_score = lax.Precision.HIGHEST
    prompt_f = prompts.astype(jnp.float32)
    normed = scaled_rows(prompt_f).astype(jnp.bfloat16)
    gate_baseline = jnp.dot(normed, gate_weight, preferred_element_type=jnp.float32).astype(jnp.bfloat16)
    up_baseline = jnp.dot(normed, up_weight, preferred_element_type=jnp.float32).astype(jnp.bfloat16)
    normed_f = normed.astype(jnp.float32)
    in_scale = 0.2 / math.sqrt(D)
    lowrank_gate = (in_scale * jnp.einsum('rd,mdk->mrk', normed_f, gate_in.astype(jnp.float32), precision=highest_score)).astype(jnp.bfloat16)
    lowrank_up = (in_scale * jnp.einsum('rd,mdk->mrk', normed_f, up_in.astype(jnp.float32), precision=highest_score)).astype(jnp.bfloat16)
    gate_activation = gate_baseline.astype(jnp.float32)[None] + jnp.einsum('hvw,hpw->hvp', lowrank_gate.astype(jnp.float32), gate_output_factors.astype(jnp.float32), precision=highest_score)
    upper_bound = up_baseline.astype(jnp.float32)[None] + jnp.einsum('hvw,hpw->hvp', lowrank_up.astype(jnp.float32), up_output_factors.astype(jnp.float32), precision=highest_score)
    hidden_state = (jax.nn.silu(gate_activation) * upper_bound).astype(jnp.bfloat16)
    lowrank_down = 0.2 / math.sqrt(HIDDEN_UNITS_PART) * jnp.einsum('lpq,lqb->lpb', hidden_state.astype(jnp.float32), down_input_factors.astype(jnp.float32), precision=highest_score)
    members = hidden_state.shape[0]
    entry_point = jnp.dot(hidden_state.reshape(members * ROWS, HIDDEN_UNITS_PART), down_weight_matrix, preferred_element_type=jnp.float32).reshape(members, ROWS, D)
    output = prompt_f[None] + entry_point + jnp.einsum('mrk,mdk->mrd', lowrank_down, down_out.astype(jnp.float32), precision=highest_score)
    final = scaled_rows(output).astype(jnp.bfloat16)
    logits = jnp.dot(final.reshape(members * ROWS, D), label_head, preferred_element_type=jnp.float32).reshape(members, ROWS, LABELS)
    picks = targets[:, None] == jnp.arange(LABELS, dtype=jnp.int32)[None, :]
    picked = lax.optimization_barrier(jnp.sum(jnp.where(picks[None], logits, 0.0), axis=-1))
    reward = lax.optimization_barrier(jnp.mean(picked - jnp.log(lax.optimization_barrier(jnp.sum(jnp.exp(logits), axis=-1))), axis=-1))
    centre = jnp.mean(reward)
    spread = jnp.mean((reward - centre) * (reward - centre))
    scores = (reward - centre) * lax.rsqrt(spread + 1e-06)
    weighted = (scores[:, None, None] * down_out.astype(jnp.float32)).astype(jnp.bfloat16)
    left = jnp.transpose(down_input_factors, (1, 0, 2)).reshape(HIDDEN_UNITS_PART, members * RANK)
    right = jnp.transpose(weighted, (1, 0, 2)).reshape(D, members * RANK)
    update = jnp.dot(left, right.T, preferred_element_type=jnp.float32) * (1.0 / math.sqrt(members * RANK))
    return (update.astype(jnp.bfloat16), scores)
```

```python
import functools
import math

import jax
import jax.numpy as jnp
from jax import lax
from jax.experimental import pallas as pl
from jax.experimental.pallas import tpu as pltpu
from jax.sharding import PartitionSpec as P

noise_scale = 0.2
norm_eps = 1e-06


def scaled_rows(values):
    return values * lax.rsqrt(jnp.mean(values * values, axis=-1, keepdims=True) + norm_eps)


def build_hidden(
    gate_baseline, up_baseline, lowrank_gate, lowrank_up, gate_output_factors, up_output_factors
):
    gate_activation = gate_baseline.astype(jnp.float32)[None] + jnp.einsum(
        "hvw,hpw->hvp", lowrank_gate, gate_output_factors, preferred_element_type=jnp.float32
    )
    upper_bound = up_baseline.astype(jnp.float32)[None] + jnp.einsum(
        "hvw,hpw->hvp", lowrank_up, up_output_factors, preferred_element_type=jnp.float32
    )
    return (jax.nn.silu(gate_activation) * upper_bound).astype(jnp.bfloat16)


def label_terms(logits, targets):
    labels = logits.shape[1]
    picks = targets[:, None] == jnp.arange(labels, dtype=jnp.int32)[None, :]
    picked = jnp.sum(jnp.where(picks, logits, 0.0), axis=1)
    return picked - jnp.log(jnp.sum(jnp.exp(logits), axis=1))


def body(
    prompts,
    gate_weight,
    up_weight,
    down_weight_matrix,
    gate_in,
    gate_output_factors,
    up_in,
    up_output_factors,
    down_input_factors,
    down_out,
    label_head,
    targets,
):
    member = lax.axis_index("pop")
    width = prompts.shape[1]
    in_block = gate_weight.shape[0]
    ffn_half = gate_output_factors.shape[1]
    total_ff = ffn_half * lax.axis_size("tensor")
    members = down_input_factors.shape[0]
    rank = down_input_factors.shape[2]
    prompt_f = prompts.astype(jnp.float32)
    normed = scaled_rows(prompt_f).astype(jnp.bfloat16)
    own_cols = lax.dynamic_slice_in_dim(normed, member * in_block, in_block, 1)
    part_gate = jnp.dot(own_cols, gate_weight, preferred_element_type=jnp.float32)
    part_up = jnp.dot(own_cols, up_weight, preferred_element_type=jnp.float32)
    total_gate, total_up = lax.psum((part_gate, part_up), "pop")
    gate_baseline = total_gate.astype(jnp.bfloat16)
    up_baseline = total_up.astype(jnp.bfloat16)
    in_scale = noise_scale / math.sqrt(width)
    lowrank_gate = (
        in_scale * jnp.einsum("rd,mdk->mrk", normed, gate_in, preferred_element_type=jnp.float32)
    ).astype(jnp.bfloat16)
    lowrank_up = (
        in_scale * jnp.einsum("rd,mdk->mrk", normed, up_in, preferred_element_type=jnp.float32)
    ).astype(jnp.bfloat16)
    down_scale = noise_scale / math.sqrt(total_ff)
    hidden_state = build_hidden(
        gate_baseline, up_baseline, lowrank_gate, lowrank_up, gate_output_factors, up_output_factors
    )
    hidden_portion = lax.all_gather(hidden_state, "pop", axis=0, tiled=True)
    out_piece = down_out.astype(jnp.float32)
    entry_point = jnp.einsum(
        "uaz,zh->uah", hidden_portion, down_weight_matrix, preferred_element_type=jnp.float32
    )
    low_part = down_scale * jnp.einsum(
        "lpq,lqb->lpb", hidden_portion, down_input_factors, preferred_element_type=jnp.float32
    )
    partial_rows = entry_point + jnp.einsum(
        "mrk,mdk->mrd", low_part, out_piece, precision=lax.Precision.HIGHEST
    )
    rows_here = lax.all_to_all(partial_rows, "pop", split_axis=0, concat_axis=2, tiled=True)
    summed = lax.psum(rows_here, "tensor")[0]
    output = prompt_f + summed
    final = scaled_rows(output).astype(jnp.bfloat16)
    half = label_head.shape[0]
    own_half = lax.dynamic_slice_in_dim(final, lax.axis_index("tensor") * half, half, 1)
    logits = lax.psum(jnp.dot(own_half, label_head, preferred_element_type=jnp.float32), "tensor")
    reward = jnp.mean(label_terms(logits, targets))
    rewards = lax.all_gather(reward.reshape(1), "pop", axis=0, tiled=True)
    centre = jnp.mean(rewards)
    spread = jnp.mean((rewards - centre) * (rewards - centre))
    scores = (rewards - centre) * lax.rsqrt(spread + norm_eps)
    weighted = (scores[:, None, None] * down_out.astype(jnp.float32)).astype(jnp.bfloat16)
    update = jnp.einsum(
        "mfk,mdk->fd", down_input_factors, weighted, preferred_element_type=jnp.float32
    ) * (1.0 / math.sqrt(members * rank))
    own_score = lax.dynamic_slice_in_dim(scores, member, 1, 0)
    return (update.astype(jnp.bfloat16), own_score)


BF = jnp.bfloat16
F32 = jnp.float32
HI = lax.Precision.HIGHEST
NT = (((1,), (1,)), ((), ()))
TN = (((0,), (0,)), ((), ()))


def pair_kernel(
    pop, total_ff,
    prompts, gate_w, up_w, down_w, gate_in, gof, up_in, uof, dif, dout, head, targets,
    weighted_out, score_out,
    wg, wu, dw, normed, fbuild, fac, low, part, ysum, ysend, yrecv, zsend, zrecv, base,
    lhs_g, lhs_u, hid, acc, lowd, difb, xsend, xrecv, hloc, hrem, hsel,
    lsend, lrecv, csend, crecv, rbuf,
    wsem, dsem, hsem, ssem, rsem,
):
    rows, width = prompts.shape
    block, ff = gate_w.shape
    outer = pop // 2
    chunk = wg.shape[2]
    members = pop
    rank = gof.shape[0]
    half = block // 2
    labels = head.shape[1]
    over = pop * chunk - ff
    me = lax.axis_index("pop")
    core = lax.axis_index("tensor")
    z = me // 2
    y = me % 2
    sib = {"tensor": 1 - core}

    def spot(zz, yy):
        return zz * 2 + yy

    def start_of(c):
        return pl.multiple_of(c * chunk - (c // (pop - 1)) * over, 128)

    def remote(src, dst, idx, dev):
        return pltpu.make_async_remote_copy(
            src_ref=src, dst_ref=dst, send_sem=ssem.at[idx], recv_sem=rsem.at[idx],
            device_id=dev, device_id_type=pl.DeviceIdType.MESH,
        )

    owners = [spot((z + 1 + i % outer) % outer, (1 - y) if i < outer else y) for i in range(pop)]
    loads = []
    for i in range(pop):
        cols = pl.ds(start_of(owners[i]), chunk)
        a = pltpu.make_async_copy(gate_w.at[:, cols], wg.at[i], wsem.at[2 * i])
        b = pltpu.make_async_copy(up_w.at[:, cols], wu.at[i], wsem.at[2 * i + 1])
        a.start()
        b.start()
        loads.append((a, b))
    hoff = (me % (pop // 2)) * block
    hcopy = pltpu.make_async_copy(head.at[pl.ds(pl.multiple_of(hoff + core * half, half), half)], hloc, hsem)
    hcopy.start()

    barrier = pltpu.get_barrier_semaphore()
    for k in range(1, pop):
        pl.semaphore_signal(barrier, inc=1, device_id={"pop": (me + k) % pop}, device_id_type=pl.DeviceIdType.MESH)
    pl.semaphore_signal(barrier, inc=1, device_id=sib, device_id_type=pl.DeviceIdType.MESH)

    fbuild[0:rank, :] = gof[...].astype(F32)
    fbuild[rank : 2 * rank, :] = uof[...].astype(F32)
    fac[me] = fbuild[...].astype(BF)
    pl.semaphore_wait(barrier, pop)

    pending = []
    FAC, LOWI, YI, ZI, AGI, XI, HEADI, LI, CI, RI = 0, 8, 16, 20, 24, 32, 33, 34, 42, 43
    fcopies = {}
    for k in range(1, outer):
        d = remote(fac.at[me], fac.at[me], FAC + k, {"pop": spot((z + k) % outer, y)})
        d.start()
        fcopies[k] = d
        pending.append(d)
    d = remote(fac.at[me], fac.at[me], FAC + outer, {"pop": spot(z, 1 - y)})
    d.start()
    fcopies[outer] = d
    pending.append(d)
    hs = remote(
        head.at[pl.ds(pl.multiple_of(hoff + (1 - core) * half, half), half)], hrem, HEADI, sib
    )
    hs.start()
    pending.append(hs)

    x = prompts[...].astype(F32)
    normed[...] = (x * lax.rsqrt(jnp.mean(x * x, axis=-1, keepdims=True) + norm_eps)).astype(BF)

    scale = noise_scale / math.sqrt(width)
    lg = (scale * lax.dot_general(normed[...], gate_in[...], NT, preferred_element_type=F32)).astype(BF)
    lu = (scale * lax.dot_general(normed[...], up_in[...], NT, preferred_element_type=F32)).astype(BF)
    krow = lax.broadcasted_iota(jnp.int32, (rank, 128), 0)
    lane = lax.broadcasted_iota(jnp.int32, (rank, 128), 1)
    sel_g = (lane == me * 2 * rank + krow).astype(F32).astype(BF)
    sel_u = (lane == me * 2 * rank + rank + krow).astype(F32).astype(BF)
    low[me] = (
        jnp.dot(lg, sel_g, preferred_element_type=F32) + jnp.dot(lu, sel_u, preferred_element_type=F32)
    ).astype(BF)
    lcopies = []
    for k in range(1, pop):
        d = remote(low.at[me], low.at[me], LOWI + k, {"pop": (me + k) % pop})
        d.start()
        lcopies.append(d)
        pending.append(d)

    ycopies = []
    zcopies = []
    dloads = []
    xcols = pl.ds(pl.multiple_of(me * block, block), block)
    tile = 256
    for i in range(pop):
        loads[i][0].wait()
        loads[i][1].wait()
        j = i % outer
        if i >= outer:
            ycopies[j].wait_recv()

        @pl.loop(0, chunk // tile)
        def _(s, i=i, j=j):
            at = pl.ds(pl.multiple_of(s * tile, tile), tile)
            for g, w in enumerate((wg, wu)):
                got = jnp.dot(normed[:, xcols], w[i, :, at], preferred_element_type=F32)
                if i < outer:
                    ysend[j, g, :, at] = got.astype(BF)
                elif i < pop - 1:
                    zsend[j, g, :, at] = (got + yrecv[j, g, :, at].astype(F32)).astype(BF)
                else:
                    ysum[g, :, at] = got + yrecv[j, g, :, at].astype(F32)

        if i < outer:
            d = remote(ysend.at[j], yrecv.at[j], YI + j, {"pop": spot(z, 1 - y)})
            d.start()
            ycopies.append(d)
            pending.append(d)
        elif i < pop - 1:
            d = remote(zsend.at[j], zrecv.at[j], ZI + j, {"pop": spot((z + 1 + j) % outer, y)})
            d.start()
            zcopies.append(d)
            pending.append(d)
        if i == 1:
            for k in range(1, outer):
                fcopies[k].wait_recv()
                src = spot((z + outer - k) % outer, y)
                d = remote(fac.at[src], fac.at[src], FAC + outer + k, {"pop": spot(z, 1 - y)})
                d.start()
                fcopies[outer + k] = d
                pending.append(d)
        if i >= outer:
            step = ff // 4
            n = i - outer
            d = pltpu.make_async_copy(
                down_w.at[pl.ds(n * step, step)], dw.at[pl.ds(n * step, step)], dsem.at[n]
            )
            d.start()
            dloads.append(d)

    total = [ysum[0], ysum[1]]
    for j in range(outer - 1):
        zcopies[j].wait_recv()
        for g in range(2):
            total[g] = total[g] + zrecv[j, g].astype(F32)
    for g in range(2):
        base[0, g] = total[g].astype(BF)

    acopies = {}
    d = remote(base.at[0], base.at[outer], AGI + outer, {"pop": spot(z, 1 - y)})
    d.start()
    acopies[outer] = d
    pending.append(d)
    for k in (2, 1, 3):
        d = remote(base.at[0], base.at[k], AGI + k, {"pop": spot((z + k) % outer, y)})
        d.start()
        acopies[k] = d
        pending.append(d)

    for d in lcopies:
        d.wait_recv()
    for k in range(outer, pop):
        fcopies[k].wait_recv()
    lhs = jnp.concatenate([low[m].astype(F32) for m in range(members)], axis=0)
    lanes = lax.broadcasted_iota(jnp.int32, lhs.shape, 1) % (2 * rank)
    lhs_g[...] = jnp.where(lanes < rank, lhs, 0.0).astype(BF)
    lhs_u[...] = jnp.where(lanes >= rank, lhs, 0.0).astype(BF)
    kk = 2 * rank * members
    for m in range(members):
        difb[m * rank : (m + 1) * rank, :] = dif[m].astype(F32)
    acc[...] = jnp.zeros_like(acc)
    lowd[...] = jnp.zeros_like(lowd)

    def expand(slot, c):
        start = start_of(c)
        skip = (c // (pop - 1)) * over

        @pl.loop(0, chunk // tile)
        def _(s):
            off = pl.multiple_of(s * tile, tile)
            at = pl.ds(pl.multiple_of(start + off, 128), tile)
            f = jnp.concatenate([fac[m, :, at].astype(F32) for m in range(members)], axis=0).astype(BF)
            gate = jnp.dot(lhs_g[:, :kk], f, preferred_element_type=F32)
            up = jnp.dot(lhs_u[:, :kk], f, preferred_element_type=F32)
            bg = base[slot, 0, :, pl.ds(off, tile)].astype(F32)
            bu = base[slot, 1, :, pl.ds(off, tile)].astype(F32)
            gate = gate + jnp.concatenate([bg] * members, axis=0)
            up = up + jnp.concatenate([bu] * members, axis=0)
            h = gate * (0.5 + 0.5 * jnp.tanh(0.5 * gate)) * up
            col = lax.broadcasted_iota(jnp.int32, h.shape, 1) + off
            hid[:, pl.ds(off, tile)] = jnp.where(col >= skip, h, 0.0).astype(BF)

        lowd[...] += lax.dot_general(
            hid[...], difb[:, pl.ds(start, chunk)].astype(BF), NT, preferred_element_type=F32
        )

        @pl.loop(0, block // tile)
        def _(s):
            at = pl.ds(pl.multiple_of(s * tile, tile), tile)
            acc[:, at] += jnp.dot(hid[...], dw[pl.ds(start, chunk), at], preferred_element_type=F32)

    for d in dloads:
        d.wait()
    expand(0, me)
    acopies[outer].wait_recv()
    expand(outer, spot(z, 1 - y))
    for k in (1, 2, 3):
        acopies[k].wait_recv()
        d = remote(base.at[k], base.at[outer + k], AGI + outer + k, {"pop": spot(z, 1 - y)})
        d.start()
        acopies[outer + k] = d
        pending.append(d)
        expand(k, spot((z + outer - k) % outer, y))
    for k in (1, 2, 3):
        acopies[outer + k].wait_recv()
        expand(outer + k, spot((z + outer - k) % outer, 1 - y))

    mine = lax.broadcasted_iota(jnp.int32, lowd.shape, 0) // rows == lax.broadcasted_iota(jnp.int32, lowd.shape, 1) // rank
    lowm = jnp.where(mine, lowd[...] * (noise_scale / math.sqrt(total_ff)), 0.0)
    for m in range(members):
        fbuild[0:rank, 0:block] = dout[m].astype(F32)
        weighted_out[m * rank : (m + 1) * rank, :] = fbuild[0:rank, 0:block]
    acc[...] += jnp.dot(lowm, weighted_out[...], preferred_element_type=F32, precision=HI)

    theirs = pl.ds(pl.multiple_of((1 - core) * half, half), half)
    ours = pl.ds(pl.multiple_of(core * half, half), half)
    xsend[...] = acc[:, theirs]
    xc = remote(xsend, xrecv, XI, sib)
    xc.start()
    pending.append(xc)
    hcopy.wait()
    hs.wait_recv()

    @pl.when(core == me // (pop // 2))
    def _():
        hsel[...] = hloc[...]

    @pl.when(core != me // (pop // 2))
    def _():
        hsel[...] = hrem[...]

    pcols = prompts[:, pl.ds(pl.multiple_of(me * block + core * half, half), half)].astype(F32)
    xc.wait_recv()
    lsend[...] = jnp.zeros_like(lsend)
    ones = jnp.ones((8, half), F32)
    out = acc[:, ours] + xrecv[...] + jnp.concatenate([pcols] * members, axis=0)
    top = out.astype(BF)
    rest = (out - top.astype(F32)).astype(BF)
    logits = jnp.dot(top, hsel[...], preferred_element_type=F32) + jnp.dot(
        rest, hsel[...], preferred_element_type=F32
    )
    squares = out * out
    for m in range(members):
        r = slice(m * rows, (m + 1) * rows)
        lsend[m, 0:rows, :] = logits[r]
        lsend[m, rows : rows + 8, 0:rows] = lax.dot_general(
            ones, squares[r], NT, preferred_element_type=F32, precision=HI
        )
    bcopies = []
    for k in range(1, pop):
        to = (me + k) % pop
        d = remote(lsend.at[to], lrecv.at[k], LI + k, {"pop": to})
        d.start()
        bcopies.append(d)
        pending.append(d)
    tot = lsend[me]
    for k in range(1, pop):
        bcopies[k - 1].wait_recv()
        tot = tot + lrecv[k]
    csend[...] = tot
    cc = remote(csend, crecv, CI, sib)
    cc.start()
    pending.append(cc)
    cc.wait_recv()
    tot = csend[...] + crecv[...]
    eye = (
        lax.broadcasted_iota(jnp.int32, (rows, labels), 0) == lax.broadcasted_iota(jnp.int32, (rows, labels), 1)
    ).astype(F32)
    ssq = jnp.sum(eye * tot[rows : rows + 1, :], axis=1, keepdims=True)
    lgt = tot[0:rows, :] * lax.rsqrt(ssq * (1.0 / width) + norm_eps)
    picks = targets[...] == lax.broadcasted_iota(jnp.int32, (rows, labels), 1)
    picked = jnp.sum(jnp.where(picks, lgt, 0.0), axis=1, keepdims=True)
    term = picked - jnp.log(jnp.sum(jnp.exp(lgt), axis=1, keepdims=True))
    reward = jnp.sum(jnp.broadcast_to(term, (rows, 128)), axis=0, keepdims=True) * (1.0 / rows)
    rbuf[me] = jnp.broadcast_to(reward, (8, 128))
    rcopies = []
    for k in range(1, pop):
        d = remote(rbuf.at[me], rbuf.at[me], RI + k, {"pop": (me + k) % pop})
        d.start()
        rcopies.append(d)
        pending.append(d)
    for d in rcopies:
        d.wait_recv()
    centre = sum(rbuf[m] for m in range(members)) * (1.0 / members)
    spread = sum((rbuf[m] - centre) * (rbuf[m] - centre) for m in range(members)) * (1.0 / members)
    inv = lax.rsqrt(spread + norm_eps)
    score_out[...] = (rbuf[me] - centre) * inv
    for m in range(members):
        sc = ((rbuf[m] - centre) * inv)[0:1, 0:1]
        r = slice(m * rank, (m + 1) * rank)
        weighted_out[r, :] = (dout[m].astype(F32) * sc).astype(BF).astype(F32)
    for d in pending:
        d.wait_send()


def update_kernel(norm, dif, weighted, out):
    members = dif.shape[0]
    left = jnp.concatenate([dif[m].astype(F32) for m in range(members)], axis=0).astype(BF)
    got = lax.dot_general(left, weighted[...].astype(BF), TN, preferred_element_type=F32)
    out[...] = (got * norm).astype(BF)


def fast_body(
    pop, prompts, gate_weight, up_weight, down_weight, gate_in, gof, up_in, uof, dif, dout, head, targets
):
    rows, width = prompts.shape
    block, ff = gate_weight.shape
    members, _, rank = dif.shape
    outer = pop // 2
    chunk = -(-(ff // 128) // pop) * 128
    labels = head.shape[1]
    swap = lambda v: jnp.swapaxes(v, 1, 2)
    dif_t, dout_t = swap(dif), swap(dout)
    vm = pl.BlockSpec(memory_space=pltpu.VMEM)
    hb = pl.BlockSpec(memory_space=pl.ANY)
    V = pltpu.VMEM
    big = members * rows
    weighted, score = pl.pallas_call(
        functools.partial(pair_kernel, pop, 2 * ff),
        out_shape=(
            jax.ShapeDtypeStruct((members * rank, block), F32),
            jax.ShapeDtypeStruct((8, 128), F32),
        ),
        in_specs=[vm, hb, hb, hb, vm, vm, vm, vm, vm, vm, hb, vm],
        out_specs=(vm, vm),
        scratch_shapes=[
            V((pop, block, chunk), BF), V((pop, block, chunk), BF), V((ff, block), BF),
            V((rows, width), BF), V((2 * rank, ff), F32), V((members, 2 * rank, ff), BF),
            V((members, rows, 128), BF), V((8, 128), F32), V((2, rows, chunk), F32),
            V((outer, 2, rows, chunk), BF), V((outer, 2, rows, chunk), BF),
            V((outer, 2, rows, chunk), BF), V((outer, 2, rows, chunk), BF),
            V((pop, 2, rows, chunk), BF),
            V((big, 128), BF), V((big, 128), BF), V((big, chunk), BF), V((big, block), F32),
            V((big, members * rank), F32), V((members * rank, ff), F32),
            V((big, block // 2), F32), V((big, block // 2), F32),
            V((block // 2, labels), BF), V((block // 2, labels), BF), V((block // 2, labels), BF),
            V((members, rows + 8, labels), F32), V((members, rows + 8, labels), F32),
            V((rows + 8, labels), F32), V((rows + 8, labels), F32), V((members, 8, 128), F32),
            pltpu.SemaphoreType.DMA((2 * pop,)), pltpu.SemaphoreType.DMA((4,)), pltpu.SemaphoreType.DMA,
            pltpu.SemaphoreType.DMA((52,)), pltpu.SemaphoreType.DMA((52,)),
        ],
        compiler_params=pltpu.CompilerParams(
            collective_id=0, has_side_effects=True, vmem_limit_bytes=66 * 1000 * 1000
        ),
        name="pair",
    )(
        prompts, gate_weight, up_weight, down_weight, swap(gate_in)[0], swap(gof)[0], swap(up_in)[0],
        swap(uof)[0], dif_t, dout_t, head, targets[:, None],
    )
    tile = 256
    update = pl.pallas_call(
        functools.partial(update_kernel, 1.0 / math.sqrt(members * rank)),
        grid=(ff // tile,),
        out_shape=jax.ShapeDtypeStruct((ff, block), BF),
        in_specs=[
            pl.BlockSpec((members, rank, tile), lambda i: (0, 0, i)),
            pl.BlockSpec((members * rank, block), lambda i: (0, 0)),
        ],
        out_specs=pl.BlockSpec((tile, block), lambda i: (i, 0)),
        name="update",
    )(dif_t, weighted)
    return update, score[0, :1]


def solution(mesh):
    placed = (
        P("groups", None),
        P("pop", "tensor"),
        P("pop", "tensor"),
        P("tensor", "pop"),
        P(("groups", "pop"), None, None),
        P(("groups", "pop"), "tensor", None),
        P(("groups", "pop"), None, None),
        P(("groups", "pop"), "tensor", None),
        P("groups", "tensor", None),
        P("groups", "pop", None),
        P("tensor", None),
        P("groups"),
    )
    pop = mesh.shape["pop"]
    run = functools.partial(fast_body, pop) if pop == 8 and mesh.shape["tensor"] == 2 else body
    return jax.shard_map(
        run,
        mesh=mesh,
        in_specs=placed,
        out_specs=(P(("groups", "tensor"), "pop"), P(("groups", "pop"))),
        check_vma=False,
    )
```

```python
import functools
import math

import jax
import jax.numpy as jnp
from jax import lax
from jax.experimental import pallas as pl
from jax.experimental.pallas import tpu as pltpu
from jax.sharding import PartitionSpec as P

noise_scale = 0.2
norm_eps = 1e-06


def scaled_rows(values):
    return values * lax.rsqrt(jnp.mean(values * values, axis=-1, keepdims=True) + norm_eps)


def build_hidden(
    gate_baseline, up_baseline, lowrank_gate, lowrank_up, gate_output_factors, up_output_factors
):
    gate_activation = gate_baseline.astype(jnp.float32)[None] + jnp.einsum(
        "hvw,hpw->hvp", lowrank_gate, gate_output_factors, preferred_element_type=jnp.float32
    )
    upper_bound = up_baseline.astype(jnp.float32)[None] + jnp.einsum(
        "hvw,hpw->hvp", lowrank_up, up_output_factors, preferred_element_type=jnp.float32
    )
    return (jax.nn.silu(gate_activation) * upper_bound).astype(jnp.bfloat16)


def label_terms(logits, targets):
    labels = logits.shape[1]
    picks = targets[:, None] == jnp.arange(labels, dtype=jnp.int32)[None, :]
    picked = jnp.sum(jnp.where(picks, logits, 0.0), axis=1)
    return picked - jnp.log(jnp.sum(jnp.exp(logits), axis=1))


def body(
    prompts,
    gate_weight,
    up_weight,
    down_weight_matrix,
    gate_in,
    gate_output_factors,
    up_in,
    up_output_factors,
    down_input_factors,
    down_out,
    label_head,
    targets,
):
    member = lax.axis_index("pop")
    width = prompts.shape[1]
    in_block = gate_weight.shape[0]
    ffn_half = gate_output_factors.shape[1]
    total_ff = ffn_half * lax.axis_size("tensor")
    members = down_input_factors.shape[0]
    rank = down_input_factors.shape[2]
    prompt_f = prompts.astype(jnp.float32)
    normed = scaled_rows(prompt_f).astype(jnp.bfloat16)
    own_cols = lax.dynamic_slice_in_dim(normed, member * in_block, in_block, 1)
    part_gate = jnp.dot(own_cols, gate_weight, preferred_element_type=jnp.float32)
    part_up = jnp.dot(own_cols, up_weight, preferred_element_type=jnp.float32)
    total_gate, total_up = lax.psum((part_gate, part_up), "pop")
    gate_baseline = total_gate.astype(jnp.bfloat16)
    up_baseline = total_up.astype(jnp.bfloat16)
    in_scale = noise_scale / math.sqrt(width)
    lowrank_gate = (
        in_scale * jnp.einsum("rd,mdk->mrk", normed, gate_in, preferred_element_type=jnp.float32)
    ).astype(jnp.bfloat16)
    lowrank_up = (
        in_scale * jnp.einsum("rd,mdk->mrk", normed, up_in, preferred_element_type=jnp.float32)
    ).astype(jnp.bfloat16)
    down_scale = noise_scale / math.sqrt(total_ff)
    hidden_state = build_hidden(
        gate_baseline, up_baseline, lowrank_gate, lowrank_up, gate_output_factors, up_output_factors
    )
    hidden_portion = lax.all_gather(hidden_state, "pop", axis=0, tiled=True)
    out_piece = down_out.astype(jnp.float32)
    entry_point = jnp.einsum(
        "uaz,zh->uah", hidden_portion, down_weight_matrix, preferred_element_type=jnp.float32
    )
    low_part = down_scale * jnp.einsum(
        "lpq,lqb->lpb", hidden_portion, down_input_factors, preferred_element_type=jnp.float32
    )
    partial_rows = entry_point + jnp.einsum(
        "mrk,mdk->mrd", low_part, out_piece, precision=lax.Precision.HIGHEST
    )
    rows_here = lax.all_to_all(partial_rows, "pop", split_axis=0, concat_axis=2, tiled=True)
    summed = lax.psum(rows_here, "tensor")[0]
    output = prompt_f + summed
    final = scaled_rows(output).astype(jnp.bfloat16)
    half = label_head.shape[0]
    own_half = lax.dynamic_slice_in_dim(final, lax.axis_index("tensor") * half, half, 1)
    logits = lax.psum(jnp.dot(own_half, label_head, preferred_element_type=jnp.float32), "tensor")
    reward = jnp.mean(label_terms(logits, targets))
    rewards = lax.all_gather(reward.reshape(1), "pop", axis=0, tiled=True)
    centre = jnp.mean(rewards)
    spread = jnp.mean((rewards - centre) * (rewards - centre))
    scores = (rewards - centre) * lax.rsqrt(spread + norm_eps)
    weighted = (scores[:, None, None] * down_out.astype(jnp.float32)).astype(jnp.bfloat16)
    update = jnp.einsum(
        "mfk,mdk->fd", down_input_factors, weighted, preferred_element_type=jnp.float32
    ) * (1.0 / math.sqrt(members * rank))
    own_score = lax.dynamic_slice_in_dim(scores, member, 1, 0)
    return (update.astype(jnp.bfloat16), own_score)


BF = jnp.bfloat16
F32 = jnp.float32
HI = lax.Precision.HIGHEST
NT = (((1,), (1,)), ((), ()))
TN = (((0,), (0,)), ((), ()))


def pair_kernel(
    pop, total_ff,
    prompts, gate_w, up_w, down_w, gate_in, gof, up_in, uof, dif, dout, head, targets,
    weighted_out, score_out, left_out,
    wg, wu, dw, normed, fbuild, fac, low, part, ysum, ysend, yrecv, zsend, zrecv, base,
    lhs_g, lhs_u, hid, acc, lowd, difb, xsend, xrecv, hloc, hrem, hsel,
    lsend, lrecv, csend, crecv, rbuf, leftv,
    wsem, dsem, hsem, ssem, rsem,
):
    rows, width = prompts.shape
    block, ff = gate_w.shape
    outer = pop // 2
    chunk = wg.shape[2]
    members = pop
    rank = gof.shape[0]
    half = block // 2
    labels = head.shape[1]
    over = pop * chunk - ff
    me = lax.axis_index("pop")
    core = lax.axis_index("tensor")
    z = me // 2
    y = me % 2
    sib = {"tensor": 1 - core}

    def spot(zz, yy):
        return zz * 2 + yy

    def start_of(c):
        return pl.multiple_of(c * chunk - (c // (pop - 1)) * over, 128)

    def remote(src, dst, idx, dev):
        return pltpu.make_async_remote_copy(
            src_ref=src, dst_ref=dst, send_sem=ssem.at[idx], recv_sem=rsem.at[idx],
            device_id=dev, device_id_type=pl.DeviceIdType.MESH,
        )

    owners = [spot((z + 1 + i % outer) % outer, (1 - y) if i < outer else y) for i in range(pop)]
    loads = []
    for i in range(pop):
        cols = pl.ds(start_of(owners[i]), chunk)
        a = pltpu.make_async_copy(gate_w.at[:, cols], wg.at[i], wsem.at[2 * i])
        b = pltpu.make_async_copy(up_w.at[:, cols], wu.at[i], wsem.at[2 * i + 1])
        a.start()
        b.start()
        loads.append((a, b))
    hoff = (me % (pop // 2)) * block
    hcopy = pltpu.make_async_copy(head.at[pl.ds(pl.multiple_of(hoff + core * half, half), half)], hloc, hsem.at[0])
    hcopy.start()

    barrier = pltpu.get_barrier_semaphore()
    for k in range(1, pop):
        pl.semaphore_signal(barrier, inc=1, device_id={"pop": (me + k) % pop}, device_id_type=pl.DeviceIdType.MESH)
    pl.semaphore_signal(barrier, inc=1, device_id=sib, device_id_type=pl.DeviceIdType.MESH)

    fbuild[0:rank, :] = gof[...].astype(F32)
    fbuild[rank : 2 * rank, :] = uof[...].astype(F32)
    fac[me] = fbuild[...].astype(BF)
    pl.semaphore_wait(barrier, pop)

    pending = []
    FAC, LOWI, YI, ZI, AGI, XI, HEADI, LI, CI, RI = 0, 8, 16, 20, 24, 32, 33, 34, 42, 43
    fcopies = {}
    for k in range(1, outer):
        d = remote(fac.at[me], fac.at[me], FAC + k, {"pop": spot((z + k) % outer, y)})
        d.start()
        fcopies[k] = d
        pending.append(d)
    hs = remote(
        head.at[pl.ds(pl.multiple_of(hoff + (1 - core) * half, half), half)], hrem, HEADI, sib
    )
    hs.start()
    pending.append(hs)

    x = prompts[...].astype(F32)
    normed[...] = (x * lax.rsqrt(jnp.mean(x * x, axis=-1, keepdims=True) + norm_eps)).astype(BF)

    scale = noise_scale / math.sqrt(width)
    lg = (scale * lax.dot_general(normed[...], gate_in[...], NT, preferred_element_type=F32)).astype(BF)
    lu = (scale * lax.dot_general(normed[...], up_in[...], NT, preferred_element_type=F32)).astype(BF)
    krow = lax.broadcasted_iota(jnp.int32, (rank, 128), 0)
    lane = lax.broadcasted_iota(jnp.int32, (rank, 128), 1)
    sel_g = (lane == me * 2 * rank + krow).astype(F32).astype(BF)
    sel_u = (lane == me * 2 * rank + rank + krow).astype(F32).astype(BF)
    low[me] = (
        jnp.dot(lg, sel_g, preferred_element_type=F32) + jnp.dot(lu, sel_u, preferred_element_type=F32)
    ).astype(BF)
    lcopies = []
    for k in range(1, pop):
        d = remote(low.at[me], low.at[me], LOWI + k, {"pop": (me + k) % pop})
        d.start()
        lcopies.append(d)
        pending.append(d)

    ycopies = []
    zcopies = []
    dloads = []
    xcols = pl.ds(pl.multiple_of(me * block, block), block)
    tile = 256
    for i in range(pop):
        loads[i][0].wait()
        loads[i][1].wait()
        j = i % outer
        if i >= outer:
            ycopies[j].wait_recv()

        @pl.loop(0, chunk // tile)
        def _(s, i=i, j=j):
            at = pl.ds(pl.multiple_of(s * tile, tile), tile)
            for g, w in enumerate((wg, wu)):
                got = jnp.dot(normed[:, xcols], w[i, :, at], preferred_element_type=F32)
                if i < outer:
                    ysend[j, g, :, at] = got.astype(BF)
                elif i < pop - 1:
                    zsend[j, g, :, at] = (got + yrecv[j, g, :, at].astype(F32)).astype(BF)
                else:
                    ysum[g, :, at] = got + yrecv[j, g, :, at].astype(F32)

        if i < outer:
            d = remote(ysend.at[j], yrecv.at[j], YI + j, {"pop": spot(z, 1 - y)})
            d.start()
            ycopies.append(d)
            pending.append(d)
        elif i < pop - 1:
            d = remote(zsend.at[j], zrecv.at[j], ZI + j, {"pop": spot((z + 1 + j) % outer, y)})
            d.start()
            zcopies.append(d)
            pending.append(d)
        if i == outer - 1:
            d = remote(fac.at[me], fac.at[me], FAC + outer, {"pop": spot(z, 1 - y)})
            d.start()
            fcopies[outer] = d
            pending.append(d)
        if i >= outer:
            step = ff // 4
            n = i - outer
            d = pltpu.make_async_copy(
                down_w.at[pl.ds(n * step, step)], dw.at[pl.ds(n * step, step)], dsem.at[n]
            )
            d.start()
            dloads.append(d)

    for k in range(1, outer):
        fcopies[k].wait_recv()
        src = spot((z + outer - k) % outer, y)
        d = remote(fac.at[src], fac.at[src], FAC + outer + k, {"pop": spot(z, 1 - y)})
        d.start()
        fcopies[outer + k] = d
        pending.append(d)

    for m in range(members):
        difb[m * rank : (m + 1) * rank, :] = dif[m].astype(F32)

    @pl.loop(0, ff // 128)
    def _(s):
        at = pl.ds(pl.multiple_of(s * 128, 128), 128)
        leftv[at, :] = difb[:, at].T.astype(BF)

    lcopy = pltpu.make_async_copy(leftv, left_out, hsem.at[1])
    lcopy.start()
    acc[...] = jnp.zeros_like(acc)
    lowd[...] = jnp.zeros_like(lowd)
    for d in lcopies:
        d.wait_recv()
    lhs = jnp.concatenate([low[m].astype(F32) for m in range(members)], axis=0)
    lanes = lax.broadcasted_iota(jnp.int32, lhs.shape, 1) % (2 * rank)
    lhs_g[...] = jnp.where(lanes < rank, lhs, 0.0).astype(BF)
    lhs_u[...] = jnp.where(lanes >= rank, lhs, 0.0).astype(BF)
    for d in dloads:
        d.wait()

    total = [ysum[0], ysum[1]]
    for j in range(outer - 1):
        zcopies[j].wait_recv()
        for g in range(2):
            total[g] = total[g] + zrecv[j, g].astype(F32)
    for g in range(2):
        base[0, g] = total[g].astype(BF)

    acopies = {}
    d = remote(base.at[0], base.at[outer], AGI + outer, {"pop": spot(z, 1 - y)})
    d.start()
    acopies[outer] = d
    pending.append(d)
    for k in (2, 1, 3):
        d = remote(base.at[0], base.at[k], AGI + k, {"pop": spot((z + k) % outer, y)})
        d.start()
        acopies[k] = d
        pending.append(d)

    for k in range(outer, pop):
        fcopies[k].wait_recv()
    kk = 2 * rank * members

    def expand(slot, c):
        start = start_of(c)
        skip = (c // (pop - 1)) * over

        @pl.loop(0, chunk // tile)
        def _(s):
            off = pl.multiple_of(s * tile, tile)
            at = pl.ds(pl.multiple_of(start + off, 128), tile)
            f = jnp.concatenate([fac[m, :, at].astype(F32) for m in range(members)], axis=0).astype(BF)
            gate = jnp.dot(lhs_g[:, :kk], f, preferred_element_type=F32)
            up = jnp.dot(lhs_u[:, :kk], f, preferred_element_type=F32)
            bg = base[slot, 0, :, pl.ds(off, tile)].astype(F32)
            bu = base[slot, 1, :, pl.ds(off, tile)].astype(F32)
            gate = gate + jnp.concatenate([bg] * members, axis=0)
            up = up + jnp.concatenate([bu] * members, axis=0)
            h = gate * (0.5 + 0.5 * jnp.tanh(0.5 * gate)) * up
            col = lax.broadcasted_iota(jnp.int32, h.shape, 1) + off
            hid[:, pl.ds(off, tile)] = jnp.where(col >= skip, h, 0.0).astype(BF)

        lowd[...] += lax.dot_general(
            hid[...], difb[:, pl.ds(start, chunk)].astype(BF), NT, preferred_element_type=F32
        )

        @pl.loop(0, block // tile)
        def _(s):
            at = pl.ds(pl.multiple_of(s * tile, tile), tile)
            acc[:, at] += jnp.dot(hid[...], dw[pl.ds(start, chunk), at], preferred_element_type=F32)

    expand(0, me)
    acopies[outer].wait_recv()
    expand(outer, spot(z, 1 - y))
    for k in (1, 2, 3):
        acopies[k].wait_recv()
        d = remote(base.at[k], base.at[outer + k], AGI + outer + k, {"pop": spot(z, 1 - y)})
        d.start()
        acopies[outer + k] = d
        pending.append(d)
        expand(k, spot((z + outer - k) % outer, y))
    for k in (1, 2, 3):
        acopies[outer + k].wait_recv()
        expand(outer + k, spot((z + outer - k) % outer, 1 - y))

    mine = lax.broadcasted_iota(jnp.int32, lowd.shape, 0) // rows == lax.broadcasted_iota(jnp.int32, lowd.shape, 1) // rank
    lowm = jnp.where(mine, lowd[...] * (noise_scale / math.sqrt(total_ff)), 0.0)
    for m in range(members):
        fbuild[0:rank, 0:block] = dout[m].astype(F32)
        weighted_out[m * rank : (m + 1) * rank, :] = fbuild[0:rank, 0:block]
    acc[...] += jnp.dot(lowm, weighted_out[...], preferred_element_type=F32, precision=HI)

    theirs = pl.ds(pl.multiple_of((1 - core) * half, half), half)
    ours = pl.ds(pl.multiple_of(core * half, half), half)
    xsend[...] = acc[:, theirs]
    xc = remote(xsend, xrecv, XI, sib)
    xc.start()
    pending.append(xc)
    hcopy.wait()
    hs.wait_recv()

    @pl.when(core == me // (pop // 2))
    def _():
        hsel[...] = hloc[...]

    @pl.when(core != me // (pop // 2))
    def _():
        hsel[...] = hrem[...]

    pcols = prompts[:, pl.ds(pl.multiple_of(me * block + core * half, half), half)].astype(F32)
    xc.wait_recv()
    lsend[...] = jnp.zeros_like(lsend)
    ones = jnp.ones((8, half), F32)
    out = acc[:, ours] + xrecv[...] + jnp.concatenate([pcols] * members, axis=0)
    top = out.astype(BF)
    rest = (out - top.astype(F32)).astype(BF)
    logits = jnp.dot(top, hsel[...], preferred_element_type=F32) + jnp.dot(
        rest, hsel[...], preferred_element_type=F32
    )
    squares = out * out
    for m in range(members):
        r = slice(m * rows, (m + 1) * rows)
        lsend[m, 0:rows, :] = logits[r]
        lsend[m, rows : rows + 8, 0:rows] = lax.dot_general(
            ones, squares[r], NT, preferred_element_type=F32, precision=HI
        )
    bcopies = []
    for k in range(1, pop):
        to = (me + k) % pop
        d = remote(lsend.at[to], lrecv.at[k], LI + k, {"pop": to})
        d.start()
        bcopies.append(d)
        pending.append(d)
    tot = lsend[me]
    for k in range(1, pop):
        bcopies[k - 1].wait_recv()
        tot = tot + lrecv[k]
    csend[...] = tot
    cc = remote(csend, crecv, CI, sib)
    cc.start()
    pending.append(cc)
    cc.wait_recv()
    tot = csend[...] + crecv[...]
    eye = (
        lax.broadcasted_iota(jnp.int32, (rows, labels), 0) == lax.broadcasted_iota(jnp.int32, (rows, labels), 1)
    ).astype(F32)
    ssq = jnp.sum(eye * tot[rows : rows + 1, :], axis=1, keepdims=True)
    lgt = tot[0:rows, :] * lax.rsqrt(ssq * (1.0 / width) + norm_eps)
    spread_t = jnp.where(eye[:, :rows] > 0.0, jnp.broadcast_to(targets[...].astype(F32), (rows, rows)), 0.0)
    target = jnp.sum(spread_t, axis=1, keepdims=True).astype(jnp.int32)
    picks = target == lax.broadcasted_iota(jnp.int32, (rows, labels), 1)
    picked = jnp.sum(jnp.where(picks, lgt, 0.0), axis=1, keepdims=True)
    term = picked - jnp.log(jnp.sum(jnp.exp(lgt), axis=1, keepdims=True))
    reward = jnp.sum(jnp.broadcast_to(term, (rows, 128)), axis=0, keepdims=True) * (1.0 / rows)
    rbuf[me] = jnp.broadcast_to(reward, (8, 128))
    rcopies = []
    for k in range(1, pop):
        d = remote(rbuf.at[me], rbuf.at[me], RI + k, {"pop": (me + k) % pop})
        d.start()
        rcopies.append(d)
        pending.append(d)
    for d in rcopies:
        d.wait_recv()
    centre = sum(rbuf[m] for m in range(members)) * (1.0 / members)
    spread = sum((rbuf[m] - centre) * (rbuf[m] - centre) for m in range(members)) * (1.0 / members)
    inv = lax.rsqrt(spread + norm_eps)
    score_out[...] = (rbuf[me] - centre) * inv
    for m in range(members):
        sc = ((rbuf[m] - centre) * inv)[0:1, 0:1]
        r = slice(m * rank, (m + 1) * rank)
        weighted_out[r, :] = (dout[m].astype(F32) * sc).astype(BF).astype(F32)
    for d in pending:
        d.wait_send()
    lcopy.wait()


def update_kernel(norm, left, weighted, score, out, score_out):
    width = weighted.shape[1]
    rows = left[...]
    for n in range(width // 256):
        at = slice(n * 256, (n + 1) * 256)
        got = jnp.dot(rows, weighted[:, at].astype(BF), preferred_element_type=F32)
        out[:, at] = (got * norm).astype(BF)
    score_out[0] = score[0, 0]


def fast_body(
    pop, prompts, gate_weight, up_weight, down_weight, gate_in, gof, up_in, uof, dif, dout, head, targets
):
    rows, width = prompts.shape
    block, ff = gate_weight.shape
    members, _, rank = dif.shape
    outer = pop // 2
    chunk = -(-(ff // 128) // pop) * 128
    labels = head.shape[1]
    swap = lambda v: jnp.swapaxes(v, 1, 2)
    dif_t, dout_t = swap(dif), swap(dout)
    vm = pl.BlockSpec(memory_space=pltpu.VMEM)
    hb = pl.BlockSpec(memory_space=pl.ANY)
    V = pltpu.VMEM
    big = members * rows
    weighted, score, left = pl.pallas_call(
        functools.partial(pair_kernel, pop, 2 * ff),
        out_shape=(
            jax.ShapeDtypeStruct((members * rank, block), F32),
            jax.ShapeDtypeStruct((8, 128), F32),
            jax.ShapeDtypeStruct((ff, members * rank), BF),
        ),
        in_specs=[vm, hb, hb, hb, vm, vm, vm, vm, vm, vm, hb, vm],
        out_specs=(vm, vm, hb),
        scratch_shapes=[
            V((pop, block, chunk), BF), V((pop, block, chunk), BF), V((ff, block), BF),
            V((rows, width), BF), V((2 * rank, ff), F32), V((members, 2 * rank, ff), BF),
            V((members, rows, 128), BF), V((8, 128), F32), V((2, rows, chunk), F32),
            V((outer, 2, rows, chunk), BF), V((outer, 2, rows, chunk), BF),
            V((outer, 2, rows, chunk), BF), V((outer, 2, rows, chunk), BF),
            V((pop, 2, rows, chunk), BF),
            V((big, 128), BF), V((big, 128), BF), V((big, chunk), BF), V((big, block), F32),
            V((big, members * rank), F32), V((members * rank, ff), F32),
            V((big, block // 2), F32), V((big, block // 2), F32),
            V((block // 2, labels), BF), V((block // 2, labels), BF), V((block // 2, labels), BF),
            V((members, rows + 8, labels), F32), V((members, rows + 8, labels), F32),
            V((rows + 8, labels), F32), V((rows + 8, labels), F32), V((members, 8, 128), F32), V((ff, members * rank), BF),
            pltpu.SemaphoreType.DMA((2 * pop,)), pltpu.SemaphoreType.DMA((4,)), pltpu.SemaphoreType.DMA((2,)),
            pltpu.SemaphoreType.DMA((52,)), pltpu.SemaphoreType.DMA((52,)),
        ],
        compiler_params=pltpu.CompilerParams(
            collective_id=0, has_side_effects=True, vmem_limit_bytes=66 * 1000 * 1000
        ),
        name="pair",
    )(
        prompts, gate_weight, up_weight, down_weight, swap(gate_in)[0], swap(gof)[0], swap(up_in)[0],
        swap(uof)[0], dif_t, dout_t, head, targets[None],
    )
    tile = ff // 8
    update, scores = pl.pallas_call(
        functools.partial(update_kernel, 1.0 / math.sqrt(members * rank)),
        grid=(ff // tile,),
        out_shape=(jax.ShapeDtypeStruct((ff, block), BF), jax.ShapeDtypeStruct((1,), F32)),
        in_specs=[
            pl.BlockSpec((tile, members * rank), lambda i: (i, 0)),
            pl.BlockSpec((members * rank, block), lambda i: (0, 0)),
            pl.BlockSpec((8, 128), lambda i: (0, 0)),
        ],
        out_specs=(
            pl.BlockSpec((tile, block), lambda i: (i, 0)),
            pl.BlockSpec(memory_space=pltpu.SMEM),
        ),
        name="update",
    )(left, weighted, score)
    return update, scores


def solution(mesh):
    placed = (
        P("groups", None),
        P("pop", "tensor"),
        P("pop", "tensor"),
        P("tensor", "pop"),
        P(("groups", "pop"), None, None),
        P(("groups", "pop"), "tensor", None),
        P(("groups", "pop"), None, None),
        P(("groups", "pop"), "tensor", None),
        P("groups", "tensor", None),
        P("groups", "pop", None),
        P("tensor", None),
        P("groups"),
    )
    pop = mesh.shape["pop"]
    run = functools.partial(fast_body, pop) if pop == 8 and mesh.shape["tensor"] == 2 else body
    return jax.shard_map(
        run,
        mesh=mesh,
        in_specs=placed,
        out_specs=(P(("groups", "tensor"), "pop"), P(("groups", "pop"))),
        check_vma=False,
    )
```
